128 devices in a mesh: section: 8 (over z_hi, y), row: 16 (over z_lo, x, core).
Axes of the slice: x: 4, y: 4, z: 4 (z_hi: 2, z_lo: 2; z = z_hi * 2 + z_lo), core: 2. Of those that a mesh axis runs over, the one named last changes fastest.
Arguments:
- arrivals: bfloat16 [8, 512, 8192], P('section', None, 'row'), may hold values from -43 to 43
- stashed: bfloat16 [8, 512, 8192], P('section', None, 'row'), may hold values from -43 to 43
- returned: bfloat16 [8, 512, 8192], P('section', None, 'row'), may hold values from -6 to 6
- norm_gain: float32 [8, 8192], P('section'), may hold values from 0.1 to 1.9
- up_blocks: bfloat16 [8, 112, 16, 128, 128], P('section', 'row'), may hold values from -0.125 to 0.125
- up_pattern: int32 [8, 112, 16], P('section', 'row'), may hold values from 0 to 63, as said below
- down_blocks: bfloat16 [8, 112, 16, 128, 128], P('section', 'row'), may hold values from -1 to 1
- down_pattern: int32 [8, 112, 16], P('section', 'row'), may hold values from 0 to 63, as said below
Outputs:
- departing: bfloat16 [8, 512, 8192], P('section', None, 'row')
- input_grad: bfloat16 [8, 512, 8192], P('section', None, 'row')
- up_grad: float32 [8, 112, 16, 128, 128], P('section', 'row')
- down_grad: float32 [8, 112, 16, 128, 128], P('section', 'row')
- gain_grad: float32 [8, 8192], P('section', 'row')
The draws below stay inside these ranges and needn't reach their ends.
Inputs may be any that keep to these rules, and one draw needn't show every extreme that they name: `up_pattern`: in every block row of hidden units the 16 column blocks are distinct. `down_pattern`: in every block row of hidden units the 16 column blocks are distinct.
All inputs are finite; a program needn't handle non-finite values.
Results may differ from the reference program's by a relative error of at most 0.011.
Values may be sent and summed in bfloat16 or wider, within the bound.
No kernel may reach another device: no remote copies, remote signals or barrier semaphores. Data moves between devices by JAX's collectives and lax.ppermute only.
A program may use at most 256 MiB of HBM per device.

```python
import jax
import jax.numpy as jnp
from jax import lax

D = 8192
FF = 14336
BLOCK = 128
TOK = 512
SECTIONS = 8
DB = 64
FFB = 112
PER_ROW = 16


def pattern_draw(key):
    scores = jax.random.randint(key, (SECTIONS, FFB, DB), 0, 1 << 20) * DB + jnp.arange(DB, dtype=jnp.int32)
    return lax.top_k(scores, PER_ROW)[1].astype(jnp.int32)


def field_draw(key):
    first, second, third = jax.random.split(key, 3)
    base = jnp.clip(jax.random.normal(first, (SECTIONS, TOK, D), jnp.float32), -4.0, 4.0)
    rowscale = 10.0 ** (0.5 * jax.random.uniform(second, (SECTIONS, TOK, 1), jnp.float32))
    ramp = jnp.arange(D, dtype=jnp.float32) / D
    colscale = 10.0 ** (0.5 * ramp + 0.5 * jax.random.uniform(third, (SECTIONS, 1, D), jnp.float32))
    return (base * rowscale * colscale / 3.0).astype(jnp.bfloat16)


def draw_arrivals(key, part):
    return field_draw(jax.random.fold_in(key, 101))


def draw_stashed(key, part):
    return field_draw(jax.random.fold_in(key, 202))


def draw_returned(key, part):
    folded = jax.random.fold_in(key, 505)
    key_noise, key_size, key_signs = jax.random.split(folded, 3)
    noise = jnp.clip(jax.random.normal(key_noise, (SECTIONS, TOK, D), jnp.float32), -4.0, 4.0)
    magnitude = jax.random.uniform(key_size, (SECTIONS, TOK, 1), jnp.float32, 0.5, 1.5)
    signs = jnp.where(jax.random.normal(key_signs, (SECTIONS, TOK, 1), jnp.float32) >= 0.0, 1.0, -1.0)
    return (noise + signs * magnitude).astype(jnp.bfloat16)


def draw_down_blocks(key, part):
    folded = jax.random.fold_in(key, 606)
    shape_all = (SECTIONS, FFB, PER_ROW, BLOCK, BLOCK)
    spread = (FF // 4) ** (-0.5)
    offset = 0.5 / (PER_ROW * BLOCK)
    noise = jnp.clip(jax.random.normal(folded, shape_all, jnp.float32), -4.0, 4.0)
    return (noise * spread + offset).astype(jnp.bfloat16)


def draw_up_pattern(key, part):
    return pattern_draw(jax.random.fold_in(key, 303))


def draw_down_pattern(key, part):
    return pattern_draw(jax.random.fold_in(key, 404))


def steps_of(stream_key, dims, pieces, smallest, largest):
    loudness = 1.0
    for dim, parts in pieces:
        steps = jax.random.uniform(jax.random.fold_in(jax.random.fold_in(stream_key, 6), dim), (parts,), jnp.float32, smallest / len(pieces), largest / len(pieces))
        loudness = loudness * jnp.repeat(jnp.exp(steps), dims[dim] // parts).reshape((-1,) + (1,) * (len(dims) - 1 - dim))
    return loudness


def scatter_about(stream_key, shape, scale, most, cuts=(), kind=jnp.bfloat16):
    level = steps_of(stream_key, shape, cuts, -0.22, 0.18) if cuts else 1.0
    values = jax.random.normal(stream_key, shape, jnp.float32) * scale * level
    return jnp.minimum(jnp.maximum(values, -most), most).astype(kind)


def setup_inputs(seed: int = 0) -> dict:
    keys = jax.random.split(jax.random.key(seed), 9)
    return {
        "arrivals": draw_arrivals(jax.random.fold_in(keys[8], 71), 0),
        "stashed": draw_stashed(jax.random.fold_in(keys[8], 71), 0),
        "returned": draw_returned(jax.random.fold_in(keys[8], 71), 0),
        "norm_gain": jnp.clip(1.0 + 0.18 * jax.random.normal(keys[3], (SECTIONS, D), jnp.float32), 0.1, 1.9),
        "up_blocks": scatter_about(keys[4], (SECTIONS, FFB, PER_ROW, BLOCK, BLOCK), (PER_ROW * BLOCK) ** -0.5, 0.125, ((0, 8), (1, 16))),
        "up_pattern": draw_up_pattern(jax.random.fold_in(keys[8], 71), 0),
        "down_blocks": draw_down_blocks(jax.random.fold_in(keys[8], 71), 0),
        "down_pattern": draw_down_pattern(jax.random.fold_in(keys[8], 71), 0),
    }


EPSILON = 1e-05

def pick_blocks(whole, pattern):
    count = whole.shape[0]
    split = whole.reshape(count, D // BLOCK, BLOCK)
    picked = jnp.take(split, pattern.reshape(-1), axis=1)
    return picked.reshape(count, pattern.shape[0], pattern.shape[1], BLOCK)

def place_blocks(contrib, pattern):
    count = contrib.shape[0]
    flat = contrib.reshape(count, -1, BLOCK)
    total = jnp.zeros((count, D // BLOCK, BLOCK), jnp.float32).at[:, pattern.reshape(-1), :].add(flat)
    return total.reshape(count, D)

def norm_rows(features, gain):
    values = features.astype(jnp.float32)
    scale = lax.rsqrt(lax.optimization_barrier(jnp.sum(values * values, axis=1, keepdims=True)) / D + EPSILON)
    return ((values * scale * gain).astype(jnp.bfloat16), scale)

def one_section(packed):
    inward, stash, grad_out, gain, up_b, up_p, down_b, down_p = packed
    up_f = up_b.astype(jnp.float32)
    down_f = down_b.astype(jnp.float32)
    normed, scale_fwd = norm_rows(inward, gain)
    hidden = jnp.einsum('tfpb,fpcb->tfc', pick_blocks(normed, up_p).astype(jnp.float32), up_f)
    active = jax.nn.silu(hidden).astype(jnp.bfloat16)
    contrib = jnp.einsum('tfc,fpce->tfpe', active.astype(jnp.float32), down_f)
    departing = (inward.astype(jnp.float32) + place_blocks(contrib, down_p)).astype(jnp.bfloat16)
    normed_b, scale_bwd = norm_rows(stash, gain)
    picked_b = pick_blocks(normed_b, up_p).astype(jnp.float32)
    hidden_b = jnp.einsum('tfpb,fpcb->tfc', picked_b, up_f)
    sigma = jax.nn.sigmoid(hidden_b)
    active_b = (hidden_b * sigma).astype(jnp.bfloat16)
    grad_pick = pick_blocks(grad_out, down_p).astype(jnp.float32)
    grad_act = jnp.einsum('tfpe,fpce->tfc', grad_pick, down_f)
    grad_hid = (grad_act * sigma * (1.0 + hidden_b * (1.0 - sigma))).astype(jnp.bfloat16)
    down_grad = jnp.einsum('tfc,tfpe->fpce', active_b.astype(jnp.float32), grad_pick)
    up_grad = jnp.einsum('tfc,tfpb->fpcb', grad_hid.astype(jnp.float32), picked_b)
    grad_norm = place_blocks(jnp.einsum('tfc,fpcb->tfpb', grad_hid.astype(jnp.float32), up_f), up_p)
    stash_f = stash.astype(jnp.float32)
    stat = lax.optimization_barrier(jnp.sum(grad_norm * gain * stash_f, axis=1, keepdims=True))
    input_grad = grad_out.astype(jnp.float32) + scale_bwd * gain * grad_norm - stash_f * (scale_bwd * scale_bwd * scale_bwd) * stat / D
    gain_grad = lax.optimization_barrier(jnp.sum(grad_norm * stash_f * scale_bwd, axis=0))
    return (departing, input_grad.astype(jnp.bfloat16), up_grad, down_grad, gain_grad)

def reference(arrivals, stashed, returned, norm_gain, up_blocks, up_pattern, down_blocks, down_pattern):
    inward = jnp.roll(arrivals, 1, axis=0)
    grad_out = jnp.roll(returned, -1, axis=0)
    results = lax.map(one_section, (inward, stashed, grad_out, norm_gain, up_blocks, up_pattern, down_blocks, down_pattern))
    return (results[0], results[1], results[2], results[3], results[4])
```

```python
import functools

import jax
import jax.numpy as jnp
from jax import lax
from jax.experimental import pallas as pl
from jax.experimental.pallas import tpu as pltpu
from jax.sharding import PartitionSpec as P

EPSILON = 1e-05
F32 = jnp.float32
BF16 = jnp.bfloat16
ROWS = "row"
LANE_LAST = (((1,), (1,)), ((), ()))
PLAIN = (((1,), (0,)), ((), ()))
TOKENS_FIRST = (((0,), (0,)), ((), ()))


def from_behind(block, axis, distance):
    count = lax.axis_size(axis)
    return lax.ppermute(block, axis, [((i - distance) % count, i) for i in range(count)])


def params(vmem_mib):
    return pltpu.CompilerParams(vmem_limit_bytes=vmem_mib << 20)


def split_kernel(x_ref, o_ref):
    for j in range(o_ref.shape[0]):
        o_ref[j] = x_ref[:, j * 128 : (j + 1) * 128]


def to_blocks(x):
    tokens, width = x.shape
    return pl.pallas_call(
        split_kernel,
        out_shape=jax.ShapeDtypeStruct((width // 128, tokens, 128), x.dtype),
        name="to_blocks",
    )(x)


def normalise(x_ref, gain_ref, scale_ref, width):
    blocks, tokens, lanes = x_ref.shape
    chunk = 64

    @pl.loop(0, tokens // chunk)
    def _(t):
        span = pl.ds(pl.multiple_of(t * chunk, chunk), chunk)

        def square(p, total):
            v = x_ref[p, span, :].astype(F32)
            return total + v * v

        total = lax.fori_loop(0, blocks, square, jnp.zeros((chunk, lanes), F32), unroll=8)
        mean = jnp.sum(total, axis=1, keepdims=True) / width
        scale = jnp.broadcast_to(lax.rsqrt(mean + EPSILON), (chunk, lanes))
        if scale_ref is not None:
            scale_ref[span, :] = scale

        def rescale(p, carry):
            v = x_ref[p, span, :].astype(F32)
            x_ref[p, span, :] = (v * scale * gain_ref[p]).astype(BF16)
            return carry

        lax.fori_loop(0, blocks, rescale, 0, unroll=8)


def clear(ref):
    def body(p, carry):
        ref[p] = jnp.zeros(ref.shape[1:], ref.dtype)
        return carry

    lax.fori_loop(0, ref.shape[0], body, 0)


def round_out(acc_ref, o_ref):
    def body(p, carry):
        o_ref[p] = acc_ref[p].astype(o_ref.dtype)
        return carry

    lax.fori_loop(0, acc_ref.shape[0], body, 0)


def pick(ref, pattern_ref, row, count):
    return jnp.concatenate([ref[pattern_ref[row, k]] for k in range(count)], axis=1)


def place(acc_ref, pattern_ref, row, coef, w_ref, count):
    for k in range(0, count, 2):
        pair = jnp.concatenate([w_ref[0, k], w_ref[0, k + 1]], axis=1)
        terms = lax.dot_general(coef, pair, PLAIN, preferred_element_type=F32)
        acc_ref[pattern_ref[row, k]] += terms[:, :128]
        acc_ref[pattern_ref[row, k + 1]] += terms[:, 128:]


def side_by_side(w_ref, count):
    return jnp.concatenate([w_ref[0, k] for k in range(count)], axis=1)


def forward_kernel(width, up_p, down_p, x_hbm, gain_ref, up_ref, down_ref, out_ref, x_ref, acc_ref, sem):
    row = pl.program_id(0)
    count = up_ref.shape[1]

    @pl.when(row == 0)
    def _():
        load = pltpu.make_async_copy(x_hbm, x_ref, sem)
        load.start()
        clear(acc_ref)
        load.wait()
        normalise(x_ref, gain_ref, None, width)

    hidden = lax.dot_general(
        pick(x_ref, up_p, row, count), side_by_side(up_ref, count), LANE_LAST, preferred_element_type=F32
    )
    active = (hidden / (1.0 + jnp.exp(-hidden))).astype(BF16)
    place(acc_ref, down_p, row, active, down_ref, count)

    @pl.when(row == pl.num_programs(0) - 1)
    def _():
        round_out(acc_ref, out_ref)


def backward_kernel(
    width, up_p, down_p, b_hbm, g_hbm, gain_ref, up_ref, down_ref,
    out_ref, scale_ref, stat_ref, up_grad_ref, down_grad_ref, b_ref, g_ref, acc_ref, sems,
):
    row = pl.program_id(0)
    count = up_ref.shape[1]

    @pl.when(row == 0)
    def _():
        load_b = pltpu.make_async_copy(b_hbm, b_ref, sems.at[0])
        load_g = pltpu.make_async_copy(g_hbm, g_ref, sems.at[1])
        load_b.start()
        load_g.start()
        clear(acc_ref)
        stat_ref[...] = jnp.zeros_like(stat_ref)
        load_b.wait()
        normalise(b_ref, gain_ref, scale_ref, width)
        load_g.wait()

    picked = pick(b_ref, up_p, row, count)
    grads = pick(g_ref, down_p, row, count)
    hidden = lax.dot_general(picked, side_by_side(up_ref, count), LANE_LAST, preferred_element_type=F32)
    grad_act = lax.dot_general(grads, side_by_side(down_ref, count), LANE_LAST, preferred_element_type=F32)
    sigma = 1.0 / (1.0 + jnp.exp(-hidden))
    active = (hidden * sigma).astype(BF16)
    grad_hid = (grad_act * sigma * (1.0 + hidden * (1.0 - sigma))).astype(BF16)
    stat_ref[...] += grad_hid.astype(F32) * hidden
    place(acc_ref, up_p, row, grad_hid, up_ref, count)
    down_grad = lax.dot_general(active, grads, TOKENS_FIRST, preferred_element_type=F32)
    up_grad = lax.dot_general(grad_hid, picked, TOKENS_FIRST, preferred_element_type=F32)
    for k in range(count):
        down_grad_ref[0, k] = down_grad[:, k * 128 : (k + 1) * 128]
        up_grad_ref[0, k] = up_grad[:, k * 128 : (k + 1) * 128]

    @pl.when(row == pl.num_programs(0) - 1)
    def _():
        round_out(acc_ref, out_ref)


def whole(*shape):
    return pl.BlockSpec(shape, lambda i, *_: (0,) * len(shape), pipeline_mode=pl.Buffered(1))


def forward_pass(x_all, gain, up_b, up_p, down_b, down_p):
    blocks, tokens, lanes = x_all.shape
    rows, count = up_p.shape
    weights = pl.BlockSpec((1, count, lanes, lanes), lambda i, *_: (i, 0, 0, 0))
    return pl.pallas_call(
        functools.partial(forward_kernel, blocks * lanes),
        grid_spec=pltpu.PrefetchScalarGridSpec(
            num_scalar_prefetch=2,
            grid=(rows,),
            in_specs=[pl.BlockSpec(memory_space=pl.ANY), whole(blocks, 1, lanes), weights, weights],
            out_specs=whole(blocks, tokens, lanes),
            scratch_shapes=[
                pltpu.VMEM((blocks, tokens, lanes), BF16),
                pltpu.VMEM((blocks, tokens, lanes), F32),
                pltpu.SemaphoreType.DMA,
            ],
        ),
        out_shape=jax.ShapeDtypeStruct((blocks, tokens, lanes), BF16),
        compiler_params=params(60),
        name="forward_pass",
    )(up_p, down_p, x_all, gain, up_b, down_b)


def backward_pass(b_all, g_all, gain, up_b, up_p, down_b, down_p):
    blocks, tokens, lanes = b_all.shape
    rows, count = up_p.shape
    weights = pl.BlockSpec((1, count, lanes, lanes), lambda i, *_: (i, 0, 0, 0))
    anywhere = pl.BlockSpec(memory_space=pl.ANY)
    grads = jax.ShapeDtypeStruct(up_b.shape, F32)
    narrow = jax.ShapeDtypeStruct((tokens, lanes), F32)
    return pl.pallas_call(
        functools.partial(backward_kernel, blocks * lanes),
        grid_spec=pltpu.PrefetchScalarGridSpec(
            num_scalar_prefetch=2,
            grid=(rows,),
            in_specs=[anywhere, anywhere, whole(blocks, 1, lanes), weights, weights],
            out_specs=[whole(blocks, tokens, lanes), whole(tokens, lanes), whole(tokens, lanes), weights, weights],
            scratch_shapes=[
                pltpu.VMEM((blocks, tokens, lanes), BF16),
                pltpu.VMEM((blocks, tokens, lanes), BF16),
                pltpu.VMEM((blocks, tokens, lanes), F32),
                pltpu.SemaphoreType.DMA((2,)),
            ],
        ),
        out_shape=[jax.ShapeDtypeStruct((blocks, tokens, lanes), BF16), narrow, narrow, grads, grads],
        compiler_params=params(60),
        name="backward_pass",
    )(up_p, down_p, b_all, g_all, gain, up_b, down_b)


def departing_kernel(x_ref, y_ref, o_ref):
    for j in range(x_ref.shape[0]):
        o_ref[:, j * 128 : (j + 1) * 128] = (x_ref[j].astype(F32) + y_ref[j].astype(F32)).astype(BF16)


def depart(x, y):
    blocks, tokens, lanes = x.shape
    return pl.pallas_call(
        departing_kernel,
        out_shape=jax.ShapeDtypeStruct((tokens, blocks * lanes), BF16),
        name="depart",
    )(x, y)


def finish_kernel(width, b_ref, g_ref, dn_ref, gain_ref, scale_ref, stat_ref, o_ref, gain_grad_ref):
    scale = scale_ref[...]
    last = scale * scale * stat_ref[...] / width
    for j in range(b_ref.shape[0]):
        b = b_ref[j].astype(F32)
        dn = dn_ref[j].astype(F32)
        grad = g_ref[j].astype(F32) + scale * gain_ref[j] * dn - b * last
        o_ref[:, j * 128 : (j + 1) * 128] = grad.astype(BF16)
        gain_grad_ref[j] = jnp.sum(dn * b * scale, axis=0, keepdims=True)


def finish(b, g, dn, gain_part, scale, stat, width):
    blocks, tokens, lanes = b.shape
    return pl.pallas_call(
        functools.partial(finish_kernel, width),
        out_shape=[
            jax.ShapeDtypeStruct((tokens, blocks * lanes), BF16),
            jax.ShapeDtypeStruct((blocks, 1, lanes), F32),
        ],
        name="finish",
    )(b, g, dn, gain_part, scale, stat)


def per_device(arrivals, stashed, returned, norm_gain, up_blocks, up_pattern, down_blocks, down_pattern):
    up_b, up_p, down_b, down_p = up_blocks[0], up_pattern[0], down_blocks[0], down_pattern[0]
    gain = norm_gain[0].reshape(-1, 1, 128)
    b = to_blocks(stashed[0])
    g = from_behind(to_blocks(returned[0]), "section", -1)
    x = from_behind(to_blocks(arrivals[0]), "section", 1)
    width = norm_gain.shape[1]
    own = b.shape[0]
    gain_part = lax.dynamic_slice_in_dim(gain, lax.axis_index(ROWS) * own, own)
    b_all = lax.all_gather(b, ROWS, axis=0, tiled=True)
    g_all = lax.all_gather(g, ROWS, axis=0, tiled=True)
    x_all = lax.all_gather(x, ROWS, axis=0, tiled=True)
    dn_part, scale, stat_part, up_grad, down_grad = backward_pass(b_all, g_all, gain, up_b, up_p, down_b, down_p)
    dn = lax.psum_scatter(dn_part, ROWS, scatter_dimension=0, tiled=True)
    stat = lax.psum(jnp.sum(stat_part, axis=1), ROWS)
    stat = jnp.broadcast_to(stat[:, None], scale.shape)
    out_part = forward_pass(x_all, gain, up_b, up_p, down_b, down_p)
    out = lax.psum_scatter(out_part, ROWS, scatter_dimension=0, tiled=True)
    input_grad, gain_grad = finish(b, g, dn, gain_part, scale, stat, width)
    departing = depart(x, out)
    return (
        departing[None],
        input_grad[None],
        up_grad[None],
        down_grad[None],
        gain_grad.reshape(1, -1),
    )


def solution(mesh):
    return jax.shard_map(
        per_device,
        mesh=mesh,
        in_specs=(
            P("section", None, "row"),
            P("section", None, "row"),
            P("section", None, "row"),
            P("section", None),
            P("section", "row", None, None, None),
            P("section", "row", None),
            P("section", "row", None, None, None),
            P("section", "row", None),
        ),
        out_specs=(
            P("section", None, "row"),
            P("section", None, "row"),
            P("section", "row", None, None, None),
            P("section", "row", None, None, None),
            P("section", "row"),
        ),
        check_vma=False,
    )
```

```python
import functools

import jax
import jax.numpy as jnp
from jax import lax
from jax.experimental import pallas as pl
from jax.experimental.pallas import tpu as pltpu
from jax.sharding import PartitionSpec as P

EPSILON = 1e-05
F32 = jnp.float32
BF16 = jnp.bfloat16
LANE_LAST = (((1,), (1,)), ((), ()))
PLAIN = (((1,), (0,)), ((), ()))
TOKENS_FIRST = (((0,), (0,)), ((), ()))

DEPTH, RING, CORES = 2, 4, 2
OWN = 4
CHIP = CORES * OWN


def row_of(z, x, c):
    return (z % DEPTH * RING + x % RING) * CORES + c % CORES


def place_of(row):
    return row // (RING * CORES), row // CORES % RING, row % CORES


def send(block, dz=0, dx=0, dc=0):
    count = DEPTH * RING * CORES
    route = []
    for row in range(count):
        z, x, c = place_of(row)
        route.append((row, row_of(z + dz, x + dx, c + dc)))
    return lax.ppermute(block, "row", route)


def send_section(block, ds, dc):
    sections, rows = lax.axis_size("section"), lax.axis_size("row")
    route = []
    for s in range(sections):
        for row in range(rows):
            z, x, c = place_of(row)
            route.append((s * rows + row, (s + ds) % sections * rows + row_of(z, x, c + dc)))
    return lax.ppermute(block, ("section", "row"), route)


def fence(*values):
    return lax.optimization_barrier(values)


def plus(*terms):
    total = terms[0].astype(F32)
    for t in terms[1:]:
        total = total + t.astype(F32)
    return total.astype(BF16)


def gather_pieces(chip):
    behind = send(chip, dz=1)
    column = jnp.concatenate([chip, behind], axis=0)
    left = send(column, dx=1)
    right = send(column, dx=-1)
    far_left = send(left[:OWN], dx=1)
    far_right = send(right[OWN:CHIP], dx=-1)
    far = jnp.concatenate([far_left, far_right], axis=0)
    far_behind = send(far, dz=1)
    return column, right, far, far_behind, left


def scatter_sum(parts):
    far, far_behind, plus_early, minus_early, plus_late, minus_late, here, behind = parts
    far_in = send(far_behind, dz=1)
    from_left = send(plus_early, dx=1)
    from_right = send(minus_early, dx=-1)
    far_plus = send(plus(far[:OWN], far_in[:OWN]), dx=1)
    far_minus = send(plus(far[OWN:], far_in[OWN:]), dx=-1)
    late_left = send(plus(plus_late, far_plus), dx=1)
    late_right = send(plus(minus_late, far_minus), dx=-1)
    behind_in = send(plus(behind, from_left[OWN:], from_right[OWN:]), dz=1)
    return here, behind_in, from_left, late_left, from_right, late_right


def total_of(terms):
    here, behind_in, from_left, late_left, from_right, late_right = terms

    def block(j):
        total = here[j].astype(F32) + behind_in[j].astype(F32)
        if j < OWN:
            return total + late_left[j].astype(F32) + from_right[j].astype(F32)
        return total + from_left[j - OWN].astype(F32) + late_right[j - OWN].astype(F32)

    return block


PIECES = ((0, 16), (16, 16), (32, 8), (40, 8), (48, 16))
PARTS = (
    tuple(range(32, 40)),
    tuple(range(40, 48)),
    tuple(range(20, 32)),
    tuple(range(48, 52)) + tuple(range(56, 64)),
    tuple(range(16, 20)),
    tuple(range(52, 56)),
    tuple(range(0, 8)),
    tuple(range(8, 16)),
)


def params(vmem_mib=60):
    return pltpu.CompilerParams(vmem_limit_bytes=vmem_mib << 20)


ANY = pl.BlockSpec(memory_space=pl.ANY)


def whole(*shape):
    return pl.BlockSpec(shape, lambda i, *_: (0,) * len(shape), pipeline_mode=pl.Buffered(1))


def split_kernel(core, x_ref, mine_ref, other_ref):
    half = mine_ref.shape[1]
    for side, ref in ((0, mine_ref), (1, other_ref)):
        start = pl.multiple_of((core[0] ^ side) * half, half)
        for j in range(OWN):
            ref[j] = x_ref[pl.ds(start, half), j * 128 : (j + 1) * 128]


def split_tokens(x, core):
    tokens, width = x.shape
    shape = (width // 128, tokens // 2, 128)
    return pl.pallas_call(
        split_kernel,
        grid_spec=pltpu.PrefetchScalarGridSpec(
            num_scalar_prefetch=1,
            grid=(1,),
            in_specs=[whole(tokens, width)],
            out_specs=[whole(*shape)] * 2,
        ),
        out_shape=[jax.ShapeDtypeStruct(shape, x.dtype)] * 2,
        name="split_tokens",
    )(core, x)


def join_kernel(core, mine_ref, other_ref, o_ref):
    half = mine_ref.shape[1]
    for side, ref in ((0, mine_ref), (1, other_ref)):
        start = pl.multiple_of((core[0] ^ side) * half, half)
        for j in range(OWN):
            o_ref[pl.ds(start, half), j * 128 : (j + 1) * 128] = ref[j]


def join_tokens(mine, other, core):
    blocks, half, lanes = mine.shape
    return pl.pallas_call(
        join_kernel,
        grid_spec=pltpu.PrefetchScalarGridSpec(
            num_scalar_prefetch=1,
            grid=(1,),
            in_specs=[whole(*mine.shape)] * 2,
            out_specs=whole(2 * half, blocks * lanes),
        ),
        out_shape=jax.ShapeDtypeStruct((2 * half, blocks * lanes), mine.dtype),
        name="join_tokens",
    )(core, mine, other)


def normalise(x_ref, gain_ref, order_ref, scale_ref, width):
    blocks, tokens, lanes = x_ref.shape
    chunk = 64

    @pl.loop(0, tokens // chunk)
    def _(t):
        span = pl.ds(pl.multiple_of(t * chunk, chunk), chunk)

        def square(p, total):
            v = x_ref[p, span, :].astype(F32)
            return total + v * v

        total = lax.fori_loop(0, blocks, square, jnp.zeros((chunk, lanes), F32), unroll=8)
        mean = jnp.sum(total, axis=1, keepdims=True) / width
        scale = jnp.broadcast_to(lax.rsqrt(mean + EPSILON), (chunk, lanes))
        if scale_ref is not None:
            scale_ref[span, :] = scale

        def rescale(p, carry):
            v = x_ref[p, span, :].astype(F32)
            x_ref[p, span, :] = (v * scale * gain_ref[order_ref[p]]).astype(BF16)
            return carry

        lax.fori_loop(0, blocks, rescale, 0, unroll=8)


def clear(ref):
    def body(p, carry):
        ref[p] = jnp.zeros(ref.shape[1:], ref.dtype)
        return carry

    lax.fori_loop(0, ref.shape[0], body, 0, unroll=4)


def emit(acc_ref, out_refs):
    for ref, slots in zip(out_refs, PARTS):
        for n, slot in enumerate(slots):
            ref[n] = acc_ref[slot].astype(ref.dtype)


def load_pieces(pieces, ref, sem, start):
    for k, (piece, (at, size)) in enumerate(zip(pieces, PIECES)):
        copy = pltpu.make_async_copy(piece, ref.at[pl.ds(at, size)], sem.at[k])
        if start:
            copy.start()
        else:
            copy.wait()


class Weights:
    def __init__(self, own, other, buffer, sem):
        self.own, self.other, self.buffer, self.sem = own, other, buffer, sem
        self.rows = own.shape[0]

    def fetch(self, row):
        slot = lax.rem(row, 2)

        @pl.when(row < self.rows)
        def _():
            pltpu.make_async_copy(self.own.at[row], self.buffer.at[slot], self.sem.at[slot]).start()

        @pl.when((row >= self.rows) & (row < 2 * self.rows))
        def _():
            pltpu.make_async_copy(self.other.at[row - self.rows], self.buffer.at[slot], self.sem.at[slot]).start()

    def ready(self, row):
        slot = lax.rem(row, 2)
        pltpu.make_async_copy(self.own.at[0], self.buffer.at[slot], self.sem.at[slot]).wait()
        return self.buffer.at[slot]


def pick(ref, pattern_ref, row, count):
    return jnp.concatenate([ref[pattern_ref[row, k]] for k in range(count)], axis=1)


def side_by_side(w_ref, count):
    return jnp.concatenate([w_ref[k] for k in range(count)], axis=1)


def place(acc_ref, pattern_ref, row, coef, w_ref, count):
    for k in range(0, count, 2):
        pair = jnp.concatenate([w_ref[k], w_ref[k + 1]], axis=1)
        terms = lax.dot_general(coef, pair, PLAIN, preferred_element_type=F32)
        acc_ref[pattern_ref[row, k]] += terms[:, :128]
        acc_ref[pattern_ref[row, k + 1]] += terms[:, 128:]


def forward_kernel(width, up_p, down_p, order, *refs):
    pieces, refs = refs[:5], refs[5:]
    gain_ref, up_own, up_other, down_own, down_other = refs[:5]
    outs, (x_ref, acc_ref, up_buf, down_buf, sem, up_sem, down_sem) = refs[5:13], refs[13:]
    row = pl.program_id(0)
    count = up_buf.shape[1]
    up = Weights(up_own, up_other, up_buf, up_sem)
    down = Weights(down_own, down_other, down_buf, down_sem)

    @pl.when(row == 0)
    def _():
        load_pieces(pieces, x_ref, sem, True)
        up.fetch(row)
        down.fetch(row)
        clear(acc_ref)
        load_pieces(pieces, x_ref, sem, False)
        normalise(x_ref, gain_ref, order, None, width)

    up.fetch(row + 1)
    down.fetch(row + 1)
    w_up = up.ready(row)
    hidden = lax.dot_general(
        pick(x_ref, up_p, row, count), side_by_side(w_up, count), LANE_LAST, preferred_element_type=F32
    )
    active = (hidden / (1.0 + jnp.exp(-hidden))).astype(BF16)
    place(acc_ref, down_p, row, active, down.ready(row), count)

    @pl.when(row == pl.num_programs(0) - 1)
    def _():
        emit(acc_ref, outs)


def part_shapes(half):
    return [jax.ShapeDtypeStruct((len(slots), half, 128), BF16) for slots in PARTS]


def weight_buffers(count):
    return [pltpu.VMEM((2, count, 128, 128), BF16)] * 2


def forward_pass(pieces, order, gain, up, up_p, down, down_p):
    half = pieces[0].shape[1]
    blocks = gain.shape[0]
    rows, count = up_p.shape
    shapes = part_shapes(half)
    return pl.pallas_call(
        functools.partial(forward_kernel, blocks * 128),
        grid_spec=pltpu.PrefetchScalarGridSpec(
            num_scalar_prefetch=3,
            grid=(rows,),
            in_specs=[ANY] * 5 + [whole(blocks, 1, 128)] + [ANY] * 4,
            out_specs=[whole(*s.shape) for s in shapes],
            scratch_shapes=[
                pltpu.VMEM((blocks, half, 128), BF16),
                pltpu.VMEM((blocks, half, 128), F32),
                *weight_buffers(count),
                pltpu.SemaphoreType.DMA((5,)),
                pltpu.SemaphoreType.DMA((2,)),
                pltpu.SemaphoreType.DMA((2,)),
            ],
        ),
        out_shape=shapes,
        compiler_params=params(),
        name="forward_pass",
    )(up_p, down_p, order, *pieces, gain, *up, *down)


def hidden_kernel(width, up_p, order, *refs):
    pieces, refs = refs[:5], refs[5:]
    gain_ref, up_own, up_other, hidden_ref, normed_ref, scale_ref, up_buf, sem, up_sem = refs
    row = pl.program_id(0)
    count = up_buf.shape[1]
    up = Weights(up_own, up_other, up_buf, up_sem)

    @pl.when(row == 0)
    def _():
        load_pieces(pieces, normed_ref, sem, True)
        up.fetch(row)
        load_pieces(pieces, normed_ref, sem, False)
        normalise(normed_ref, gain_ref, order, scale_ref, width)

    up.fetch(row + 1)
    hidden_ref[0] = lax.dot_general(
        pick(normed_ref, up_p, row, count), side_by_side(up.ready(row), count), LANE_LAST, preferred_element_type=F32
    )


def hidden_pass(pieces, order, gain, up, up_p):
    half = pieces[0].shape[1]
    blocks = gain.shape[0]
    rows, count = up_p.shape
    return pl.pallas_call(
        functools.partial(hidden_kernel, blocks * 128),
        grid_spec=pltpu.PrefetchScalarGridSpec(
            num_scalar_prefetch=2,
            grid=(rows,),
            in_specs=[ANY] * 5 + [whole(blocks, 1, 128)] + [ANY] * 2,
            out_specs=[
                pl.BlockSpec((1, half, 128), lambda i, *_: (i, 0, 0)),
                whole(blocks, half, 128),
                whole(half, 128),
            ],
            scratch_shapes=[
                weight_buffers(count)[0],
                pltpu.SemaphoreType.DMA((5,)),
                pltpu.SemaphoreType.DMA((2,)),
            ],
        ),
        out_shape=[
            jax.ShapeDtypeStruct((rows, half, 128), F32),
            jax.ShapeDtypeStruct((blocks, half, 128), BF16),
            jax.ShapeDtypeStruct((half, 128), F32),
        ],
        compiler_params=params(),
        name="hidden_pass",
    )(up_p, order, *pieces, gain, *up)


def backward_kernel(up_p, down_p, *refs):
    pieces, refs = refs[:5], refs[5:]
    hidden_ref, up_own, up_other, down_own, down_other = refs[:5]
    outs, refs = refs[5:13], refs[13:]
    grad_ref, coef_ref, stat_ref, acc_ref, up_buf, down_buf, sem, up_sem, down_sem = refs
    row = pl.program_id(0)
    count = up_buf.shape[1]
    up = Weights(up_own, up_other, up_buf, up_sem)
    down = Weights(down_own, down_other, down_buf, down_sem)

    @pl.when(row == 0)
    def _():
        load_pieces(pieces, grad_ref, sem, True)
        up.fetch(row)
        down.fetch(row)
        clear(acc_ref)
        stat_ref[...] = jnp.zeros_like(stat_ref)
        load_pieces(pieces, grad_ref, sem, False)

    up.fetch(row + 1)
    down.fetch(row + 1)
    grad_act = lax.dot_general(
        pick(grad_ref, down_p, row, count), side_by_side(down.ready(row), count), LANE_LAST,
        preferred_element_type=F32,
    )
    hidden = hidden_ref[0]
    sigma = 1.0 / (1.0 + jnp.exp(-hidden))
    grad_hid = (grad_act * sigma * (1.0 + hidden * (1.0 - sigma))).astype(BF16)
    coef_ref[0, 0] = (hidden * sigma).astype(BF16)
    coef_ref[1, 0] = grad_hid
    stat_ref[...] += grad_hid.astype(F32) * hidden
    place(acc_ref, up_p, row, grad_hid, up.ready(row), count)

    @pl.when(row == pl.num_programs(0) - 1)
    def _():
        emit(acc_ref, outs)


def backward_pass(pieces, hidden, up, up_p, down, down_p):
    rows, half, _ = hidden.shape
    count = up_p.shape[1]
    blocks = sum(size for _, size in PIECES)
    shapes = part_shapes(half)
    return pl.pallas_call(
        backward_kernel,
        grid_spec=pltpu.PrefetchScalarGridSpec(
            num_scalar_prefetch=2,
            grid=(rows,),
            in_specs=[ANY] * 5 + [pl.BlockSpec((1, half, 128), lambda i, *_: (i, 0, 0))] + [ANY] * 4,
            out_specs=[whole(*s.shape) for s in shapes]
            + [
                whole(blocks, half, 128),
                pl.BlockSpec((2, 1, half, 128), lambda i, *_: (0, i, 0, 0)),
                whole(half, 128),
            ],
            scratch_shapes=[
                pltpu.VMEM((blocks, half, 128), F32),
                *weight_buffers(count),
                pltpu.SemaphoreType.DMA((5,)),
                pltpu.SemaphoreType.DMA((2,)),
                pltpu.SemaphoreType.DMA((2,)),
            ],
        ),
        out_shape=shapes
        + [
            jax.ShapeDtypeStruct((blocks, half, 128), BF16),
            jax.ShapeDtypeStruct((2, rows, half, 128), BF16),
            jax.ShapeDtypeStruct((half, 128), F32),
        ],
        compiler_params=params(),
        name="backward_pass",
    )(up_p, down_p, *pieces, hidden, *up, *down)


def weight_grad_kernel(up_p, down_p, coef_ref, coef_in_ref, normed, normed_in, grad, grad_in, up_ref, down_ref,
                       n0, n1, g0, g1, sem):
    row = pl.program_id(0)
    count = up_ref.shape[1]

    @pl.when(row == 0)
    def _():
        copies = [
            pltpu.make_async_copy(src, dst, sem.at[k])
            for k, (src, dst) in enumerate(((grad, g0), (grad_in, g1), (normed, n0), (normed_in, n1)))
        ]
        for copy in copies:
            copy.start()
        for copy in copies:
            copy.wait()

    for coef, pattern, mine, other, o_ref in ((0, down_p, g0, g1, down_ref), (1, up_p, n0, n1, up_ref)):
        here, there = coef_ref[coef, 0], coef_in_ref[coef, 0]
        near = jnp.concatenate([mine[pattern[row, k]] for k in range(count)], axis=1)
        far = jnp.concatenate([other[pattern[row, k] ^ OWN] for k in range(count)], axis=1)
        grads = lax.dot_general(here, near, TOKENS_FIRST, preferred_element_type=F32)
        grads = grads + lax.dot_general(there, far, TOKENS_FIRST, preferred_element_type=F32)
        for k in range(count):
            o_ref[0, k] = grads[:, k * 128 : (k + 1) * 128]


def weight_grads(coef, coef_in, normed, normed_in, grad, grad_in, up_p, down_p):
    rows, half = coef_in.shape[1:3]
    count = up_p.shape[1]
    blocks = normed.shape[0]
    weights = pl.BlockSpec((1, count, 128, 128), lambda i, *_: (i, 0, 0, 0))
    coefs = pl.BlockSpec((2, 1, half, 128), lambda i, *_: (0, i, 0, 0))
    return pl.pallas_call(
        weight_grad_kernel,
        grid_spec=pltpu.PrefetchScalarGridSpec(
            num_scalar_prefetch=2,
            grid=(rows,),
            in_specs=[coefs, coefs] + [ANY] * 4,
            out_specs=[weights, weights],
            scratch_shapes=[pltpu.VMEM((blocks, half, 128), BF16)] * 4 + [pltpu.SemaphoreType.DMA((4,))],
        ),
        out_shape=[jax.ShapeDtypeStruct((rows, count, 128, 128), F32)] * 2,
        compiler_params=params(),
        name="weight_grads",
    )(up_p, down_p, coef, coef_in, normed, normed_in, grad, grad_in)


def depart_kernel(x_ref, *refs):
    block = total_of(refs[:6])
    for j in range(CHIP):
        refs[6 + j // OWN][j % OWN] = (x_ref[j].astype(F32) + block(j)).astype(BF16)


def depart(x, terms):
    half = x.shape[1]
    return pl.pallas_call(
        depart_kernel,
        out_shape=[jax.ShapeDtypeStruct((OWN, half, 128), BF16)] * 2,
        name="depart",
    )(x, *terms)


def finish_kernel(width, b_ref, g_ref, gain_ref, scale_ref, stat_ref, *refs):
    block = total_of(refs[:6])
    outs, gain_grads = refs[6:8], refs[8:10]
    scale = scale_ref[...]
    last = scale * scale * stat_ref[...] / width
    for j in range(CHIP):
        b = b_ref[j].astype(F32)
        dn = block(j)
        grad = g_ref[j].astype(F32) + scale * gain_ref[j] * dn - b * last
        outs[j // OWN][j % OWN] = grad.astype(BF16)
        gain_grads[j // OWN][j % OWN] = jnp.sum(dn * b * scale, axis=0, keepdims=True)


def finish(b, g, gain, scale, stat, terms, width):
    half = b.shape[1]
    return pl.pallas_call(
        functools.partial(finish_kernel, width),
        out_shape=[jax.ShapeDtypeStruct((OWN, half, 128), BF16)] * 2
        + [jax.ShapeDtypeStruct((OWN, 1, 128), F32)] * 2,
        name="finish",
    )(b, g, gain, scale, stat, *terms)


def slot_of(block, z, x, c):
    dz = (block // (RING * CHIP) - z) % DEPTH
    dx = (block // CHIP - x) % RING
    dc = (block // OWN - c) % CORES
    return ((dx * DEPTH + dz) * CORES + dc) * OWN + block % OWN


def block_at(slot, z, x, c):
    dx, dz, dc = slot // (DEPTH * CHIP), slot // CHIP % DEPTH, slot // OWN % CORES
    return (((z + dz) % DEPTH * RING + (x + dx) % RING) * CORES + (c + dc) % CORES) * OWN + slot % OWN


def per_device(arrivals, stashed, returned, norm_gain, up_blocks, up_pattern, down_blocks, down_pattern):
    z, x, c = place_of(lax.axis_index("row"))
    core = jnp.reshape(c, (1,)).astype(jnp.int32)
    width = norm_gain.shape[1]
    gain = norm_gain[0].reshape(-1, 1, 128)
    own_rows = up_pattern.shape[1]

    b_mine, b_other = split_tokens(stashed[0], core)
    b_chip = jnp.concatenate([b_mine, send(b_other, dc=1)], axis=0)
    x_mine, x_other = split_tokens(arrivals[0], core)
    x_chip = jnp.concatenate([send_section(x_mine, 1, 0), send_section(x_other, 1, 1)], axis=0)
    g_mine, g_other = split_tokens(returned[0], core)
    g_chip = jnp.concatenate([send_section(g_mine, -1, 0), send_section(g_other, -1, 1)], axis=0)

    patterns = jnp.concatenate([up_pattern, down_pattern], axis=0)
    patterns = jnp.concatenate([patterns, send(patterns, dc=1)], axis=1)
    up_p, down_p = slot_of(patterns, z, x, c)
    order = block_at(jnp.arange(gain.shape[0], dtype=jnp.int32), z, x, c)
    gain_chip = lax.dynamic_slice_in_dim(gain, (z * RING + x) * CHIP, CHIP).reshape(CORES, OWN, 1, 128)
    gain_chip = jnp.where(c == 1, gain_chip[::-1], gain_chip).reshape(CHIP, 1, 128)
    up = (up_blocks[0], send(up_blocks[0], dc=1))
    down = (down_blocks[0], send(down_blocks[0], dc=1))

    b_pieces = gather_pieces(b_chip)
    g_pieces = gather_pieces(g_chip)
    x_pieces = gather_pieces(x_chip)
    hidden, normed, scale = hidden_pass(b_pieces, order, gain, up, up_p)
    normed_in = send(normed, dc=1)
    *dn_parts, grad, coef, stat = backward_pass(g_pieces, hidden, up, up_p, down, down_p)
    grad_in = send(grad, dc=1)
    coef_in = send(coef[:, own_rows:], dc=1)
    stat = jnp.sum(stat, axis=1)
    stat = stat + send(stat, dz=1)
    stat = stat + send(stat, dx=2)
    stat = stat + send(stat, dx=1)
    dn_terms = scatter_sum(dn_parts)
    out_parts = forward_pass(x_pieces, order, gain, up, up_p, down, down_p)
    out_terms = scatter_sum(out_parts)
    up_grad, down_grad = weight_grads(
        coef, coef_in, normed, normed_in, grad, grad_in, up_p[:own_rows], down_p[:own_rows]
    )
    stat = jnp.broadcast_to(stat[:, None], scale.shape)
    grad_mine, grad_other, gain_mine, gain_other = finish(b_chip, g_chip, gain_chip, scale, stat, dn_terms, width)
    input_grad = join_tokens(grad_mine, send(grad_other, dc=1), core)
    gain_grad = gain_mine + send(gain_other, dc=1)
    out_mine, out_other = depart(x_chip, out_terms)
    departing = join_tokens(out_mine, send(out_other, dc=1), core)
    return (
        departing[None],
        input_grad[None],
        up_grad[None],
        down_grad[None],
        gain_grad.reshape(1, -1),
    )


def solution(mesh):
    return jax.shard_map(
        per_device,
        mesh=mesh,
        in_specs=(
            P("section", None, "row"),
            P("section", None, "row"),
            P("section", None, "row"),
            P("section", None),
            P("section", "row", None, None, None),
            P("section", "row", None),
            P("section", "row", None, None, None),
            P("section", "row", None),
        ),
        out_specs=(
            P("section", None, "row"),
            P("section", None, "row"),
            P("section", "row", None, None, None),
            P("section", "row", None, None, None),
            P("section", "row"),
        ),
        check_vma=False,
    )
```
